32 devices in a mesh: gx: 4 (over z), gy: 8 (over y, x, core).
Axes of the slice: x: 2, y: 2, z: 4, core: 2. Of those that a mesh axis runs over, the one named last changes fastest.
Arguments:
- blocks: bfloat16 [256, 8, 256, 256], P(('gx', 'gy')), may hold values from -0.1875 to 0.1875
- block_cols: int32 [256, 8], P(('gx', 'gy')), may hold values from 0 to 23, as said below
- live_blocks: int32 [256], P(('gx', 'gy')), may hold values from 1 to 8
- send_rows: int32 [32, 4, 4], P(('gx', 'gy')), may hold values from 0 to 7, as said below
- start: float32 [256, 64, 256], P(('gx', 'gy')), may hold values from -6 to 6
- sketch: float32 [64, 256, 256], P(None, ('gx', 'gy')), may hold values from -0.0029296875 to 0.0029296875
Outputs:
- basis: float32 [4, 256, 64, 256], P(None, ('gx', 'gy'))
- factor: float32 [4, 4, 64], replicated
The draws below stay inside these ranges and needn't reach their ends.
Inputs may be any that keep to these rules, and one draw needn't show every extreme that they name: block_cols[i, 0] is block row i itself (i % 8 in the owner's numbering); only the first live_blocks[i] entries of a row are used. `send_rows`: the 4 entries of one device and direction are distinct.
All inputs are finite; a program needn't handle non-finite values.
Results may differ from the reference program's by a relative error of at most 0.0036.
Values may be sent and summed in bfloat16 or wider, within the bound.
A program may use at most 64 MiB of HBM per device.

```python
import jax
import jax.numpy as jnp
from jax import lax

BS = 256
RB = 8
KB = 8
NRHS = 64
SK = 64
STEPS = 3
H = 4
NBR = 256
NROWS = 65536
N_GX = 4
N_GY = 8
DEVICES = 32


def draw_block_cols(key, part):
    own_rows = (jnp.arange(NBR, dtype=jnp.int32) % RB)[:, None]
    others = jax.random.randint(jax.random.fold_in(key, 11), (NBR, KB - 1), 0, RB + 4 * H, dtype=jnp.int32)
    return jnp.concatenate([own_rows, others], axis=1).astype(jnp.int32)


def draw_send_rows(key, part):
    keys = jax.random.split(jax.random.fold_in(key, 7), DEVICES * 4)
    orders = jax.vmap(lambda single: jax.random.permutation(single, RB))(keys)
    return orders[:, :H].reshape(DEVICES, 4, H).astype(jnp.int32)


def plant(array, own_key, low, top_value):
    extent = array.shape
    place = [jax.random.randint(jax.random.fold_in(own_key, axis), (), 0, extent[axis]) for axis in range(len(extent))]
    array = array.at[tuple(place)].set(low)
    longest = extent.index(max(extent))
    place[longest] = (place[longest] + 1) % extent[longest]
    return array.at[tuple(place)].set(top_value)


def steps_of(stream_key, extent, cuts, low, largest):
    def one(position, blocks):
        steps = jax.random.uniform(jax.random.fold_in(jax.random.fold_in(stream_key, 6), position), (blocks,), jnp.float32, low / len(cuts), largest / len(cuts))
        return jnp.repeat(jnp.exp(steps), extent[position] // blocks).reshape((-1,) + (1,) * (len(extent) - position - 1))

    factor_of = one(*cuts[0])
    for cut in cuts[1:]:
        factor_of = factor_of * one(*cut)
    return factor_of


def scatter_about(rng, extent, width, most, cuts=(), kind=jnp.bfloat16):
    entries = width * jax.random.normal(rng, extent, jnp.float32)
    if cuts:
        entries = entries * steps_of(rng, extent, cuts, -0.22, 0.18)
    return jnp.clip(entries, -most, most).astype(kind)


def setup_inputs(seed: int = 0) -> dict:
    key_list = jax.random.split(jax.random.key(seed), 7)
    return {
        "blocks": scatter_about(key_list[0], (NBR, KB, BS, BS), (BS * KB // 2) ** -0.5, 0.1875, ((0, 32),)),
        "block_cols": draw_block_cols(jax.random.fold_in(key_list[6], 71), 0),
        "live_blocks": plant(jax.random.randint(key_list[2], (NBR,), 1, KB + 1), jax.random.fold_in(key_list[2], 1), 1, KB).astype(jnp.int32),
        "send_rows": draw_send_rows(jax.random.fold_in(key_list[6], 71), 0),
        "start": scatter_about(key_list[4], (NBR, NRHS, BS), 1.0, 6.0, ((0, 32),), jnp.float32),
        "sketch": scatter_about(key_list[5], (SK, NBR, BS), (SK * NROWS) ** -0.5, 0.0029296875, ((1, 32),), jnp.float32),
    }


def global_columns(block_cols, send_rows):
    owner = (jnp.arange(NBR, dtype=jnp.int32) // RB)[:, None]
    outer = owner // N_GY
    inner = owner % N_GY
    ghost = block_cols - RB
    direct = jnp.clip(ghost // H, 0, 3).astype(jnp.int32)
    within = (ghost % H).astype(jnp.int32)
    step_gy = jnp.where(direct == 0, -1, jnp.where(direct == 1, 1, 0))
    step_gx = jnp.where(direct == 2, -1, jnp.where(direct == 3, 1, 0))
    source = ((outer + step_gx) % N_GX * N_GY + (inner + step_gy) % N_GY).astype(jnp.int32)
    remote = source * RB + send_rows[source, direct, within]
    return jnp.where(block_cols < RB, owner * RB + block_cols, remote).astype(jnp.int32)

def power_step(vectors, columns, weights, blocks):
    rounded = vectors.astype(jnp.bfloat16)

    def one_device(pieces):
        cols, weight, block = pieces
        picked = rounded[cols].astype(jnp.float32) * weight[:, :, None, None]
        return jnp.einsum('ikrb,ikbc->irc', picked, block.astype(jnp.float32))
    result = lax.map(one_device, (columns.reshape(DEVICES, RB, KB), weights.reshape(DEVICES, RB, KB), blocks.reshape(DEVICES, RB, KB, BS, BS)))
    return result.reshape(NBR, NRHS, BS)

def orthogonalize(sketched):
    count = sketched.shape[0]
    columns = []
    factor = jnp.zeros((count, count, sketched.shape[2]), jnp.float32)
    for column in range(count):
        residue = sketched[column]
        for earlier in range(column):
            coefficient = lax.optimization_barrier(jnp.sum(columns[earlier] * sketched[column], axis=0))
            factor = factor.at[earlier, column].set(coefficient)
            residue = residue - coefficient[None, :] * columns[earlier]
        length = jnp.sqrt(lax.optimization_barrier(jnp.sum(residue * residue, axis=0)) + 1e-06)
        factor = factor.at[column, column].set(length)
        columns.append(residue / length[None, :])
    return factor

def reference(blocks, block_cols, live_blocks, send_rows, start, sketch):
    columns = global_columns(block_cols, send_rows)
    weights = (jnp.arange(KB, dtype=jnp.int32)[None, :] < live_blocks[:, None]).astype(jnp.float32)
    vectors = [start]
    for section in range(STEPS):
        vectors.append(power_step(vectors[-1], columns, weights, blocks))
    sketched = jnp.stack([jnp.einsum('sib,irb->sr', sketch, vector, precision=lax.Precision.HIGHEST) for vector in vectors])
    factor = orthogonalize(sketched)
    result = []
    for column in range(STEPS + 1):
        accum = vectors[column]
        for earlier in range(column):
            accum = accum - factor[earlier, column][None, :, None] * result[earlier]
        result.append(accum / factor[column, column][None, :, None])
    return (jnp.stack(result), factor)
```

```python
import functools

import jax
import jax.numpy as jnp
from jax import lax
from jax.experimental import pallas as pl
from jax.experimental.pallas import tpu as pltpu
from jax.sharding import PartitionSpec as P

STEPS = 3
MESH = pl.DeviceIdType.MESH
F32 = jnp.float32
BF16 = jnp.bfloat16


def contract_last(a, b):
    return lax.dot_general(a, b, (((1,), (1,)), ((), ())), preferred_element_type=F32)


def split_bf16(x):
    high = x.astype(BF16)
    low = (x - high.astype(F32)).astype(BF16)
    return high, low


def power_kernel(
    ngx,
    ngy,
    cols_hbm,
    live_hbm,
    lists_hbm,
    blocks_hbm,
    start_hbm,
    sketch_hbm,
    vecs,
    fac_out,
    cols,
    live,
    lists,
    blk,
    v0,
    sk,
    shl,
    ext0,
    ext1,
    ext2,
    outgoing,
    wsend,
    wrecv,
    gxbuf,
    fbuf,
    sem_lists,
    sem_local,
    sem_blk,
    halo_s,
    halo_r,
    p1s,
    p1r,
    p2s,
    p2r,
    p3s,
    p3r,
):
    ext = (ext0, ext1, ext2)
    rows, rhs, width = v0.shape
    slots = cols.shape[1]
    send_count = lists.shape[1]
    sk_rows = shl.shape[1] // 2
    zero_slot = ext0.shape[0] - 1
    chunk = rhs // ngy
    g, h = lax.axis_index("gx"), lax.axis_index("gy")

    scalar_loads = [
        pltpu.make_async_copy(source, target, sem_lists.at[n])
        for n, (source, target) in enumerate(
            ((lists_hbm, lists), (cols_hbm, cols), (live_hbm, live))
        )
    ]
    for load in scalar_loads:
        load.start()
    load_start = pltpu.make_async_copy(start_hbm, v0, sem_local.at[0])
    load_start.start()
    parts_wide = sk.shape[0]

    def sketch_copy(c):
        return pltpu.make_async_copy(
            sketch_hbm.at[:, pl.ds(c * 128, 128)], sk.at[c], sem_local.at[1 + c]
        )

    for c in range(parts_wide):
        sketch_copy(c).start()

    def block_copy(i):
        return pltpu.make_async_copy(blocks_hbm.at[i], blk.at[i], sem_blk.at[i])

    for i in range(rows):
        block_copy(i).start()

    barrier = pltpu.get_barrier_semaphore()
    for delta in range(1, ngy):
        pl.semaphore_signal(
            barrier, inc=1, device_id={"gy": lax.rem(h + delta, ngy)}, device_id_type=MESH
        )
    for delta in range(1, ngx):
        pl.semaphore_signal(
            barrier, inc=1, device_id={"gx": lax.rem(g + delta, ngx)}, device_id_type=MESH
        )

    for s in range(STEPS):
        ext[s][zero_slot] = jnp.zeros((rhs, width), BF16)

    targets = (
        {"gy": lax.rem(h + 1, ngy)},
        {"gy": lax.rem(h + ngy - 1, ngy)},
        {"gx": lax.rem(g + 1, ngx)},
        {"gx": lax.rem(g + ngx - 1, ngx)},
    )
    order = (2, 3, 0, 1)

    def halo_copy(s, d):
        return pltpu.make_async_remote_copy(
            src_ref=outgoing.at[s, d],
            dst_ref=ext[s].at[pl.ds(rows + d * send_count, send_count)],
            send_sem=halo_s.at[s, d],
            recv_sem=halo_r.at[s, d],
            device_id=targets[d],
            device_id_type=MESH,
        )

    def gather_outgoing(s, d):
        for j in range(send_count):
            source = v0[lists[d, j]] if s == 0 else vecs[s - 1, lists[d, j]]
            outgoing[s, d, j] = source.astype(BF16)

    def p1_copy(s, delta):
        to = lax.rem(h + delta, ngy)
        return pltpu.make_async_remote_copy(
            src_ref=wsend.at[s, to],
            dst_ref=wrecv.at[s, delta - 1],
            send_sem=p1s.at[s, delta - 1],
            recv_sem=p1r.at[s, delta - 1],
            device_id={"gy": to},
            device_id_type=MESH,
        )

    def p2_copy(s, delta):
        return pltpu.make_async_remote_copy(
            src_ref=gxbuf.at[s, g],
            dst_ref=gxbuf.at[s, g],
            send_sem=p2s.at[s, delta - 1],
            recv_sem=p2r.at[s, delta - 1],
            device_id={"gx": lax.rem(g + delta, ngx)},
            device_id_type=MESH,
        )

    def p3_copy(delta):
        return pltpu.make_async_remote_copy(
            src_ref=fbuf.at[h],
            dst_ref=fbuf.at[h],
            send_sem=p3s.at[delta - 1],
            recv_sem=p3r.at[delta - 1],
            device_id={"gy": lax.rem(h + delta, ngy)},
            device_id_type=MESH,
        )

    def sketch_of(s):
        total = jnp.zeros((2 * rhs, 2 * sk_rows), F32)
        for i in range(rows):
            value = v0[i] if s == 0 else vecs[s - 1, i]
            high, low = split_bf16(value)
            total = total + contract_last(jnp.concatenate([high, low], axis=0), shl[i])
        total = total[:rhs] + total[rhs:]
        for c in range(ngy):
            wsend[s, c] = total[c * chunk : (c + 1) * chunk]
        for delta in range(1, ngy):
            p1_copy(s, delta).start()

    def finish_gy(s):
        total = wsend[s, h]
        for delta in range(1, ngy):
            p1_copy(s, delta).wait_recv()
            total = total + wrecv[s, delta - 1]
        gxbuf[s, g] = total
        for delta in range(1, ngx):
            p2_copy(s, delta).start()

    units = []
    state = {"fac": jnp.zeros((chunk, 128), F32)}
    lane = lax.broadcasted_iota(jnp.int32, (chunk, 128), 1)

    def put(row, column, value):
        state["fac"] = jnp.where(lane == row * (STEPS + 1) + column, value, state["fac"])

    def finish_gx(s):
        for delta in range(1, ngx):
            p2_copy(s, delta).wait_recv()
        total = gxbuf[s, 0]
        for other in range(1, ngx):
            total = total + gxbuf[s, other]
        w = total[:, :sk_rows] + total[:, sk_rows:]
        residue = w
        for m in range(s):
            coefficient = jnp.sum(units[m] * w, axis=1, keepdims=True)
            put(m, s, coefficient)
            residue = residue - coefficient * units[m]
        length = jnp.sqrt(jnp.sum(residue * residue, axis=1, keepdims=True) + 1e-06)
        put(s, s, length)
        units.append(residue / length)

    for load in scalar_loads:
        load.wait()
    load_start.wait()
    for d in order:
        gather_outgoing(0, d)
    pl.semaphore_wait(barrier, ngx + ngy - 2)
    for d in order:
        halo_copy(0, d).start()
    for i in range(rows):
        ext[0][i] = v0[i].astype(BF16)

    for c in range(parts_wide):
        sketch_copy(c).wait()
        for i in range(rows):
            high, low = split_bf16(sk[c, pl.ds(i, sk_rows, stride=rows), :])
            shl[i, :, c * 128 : (c + 1) * 128] = jnp.concatenate([high, low], axis=0)
    sketch_of(0)

    for s in range(STEPS):
        for d in order:
            halo_copy(s, d).wait_recv()

        def row(i, carry):
            if s == 0:
                block_copy(i).wait()
            parts = [ext[s][i]]
            for k in range(1, slots):
                parts.append(ext[s][jnp.where(k < live[i], cols[i, k], zero_slot)])
            product = jnp.dot(
                jnp.concatenate(parts, axis=1), blk[i], preferred_element_type=F32
            )
            vecs[s, i] = product
            if s + 1 < STEPS:
                ext[s + 1][i] = product.astype(BF16)
            return carry

        lax.fori_loop(0, rows, row, 0)
        if s + 1 < STEPS:
            for d in order:
                gather_outgoing(s + 1, d)
                halo_copy(s + 1, d).start()
        sketch_of(s + 1)
        finish_gy(s)
        if s > 0:
            finish_gx(s - 1)

    finish_gx(STEPS - 1)
    finish_gy(STEPS)
    finish_gx(STEPS)
    fbuf[h] = state["fac"]
    for delta in range(1, ngy):
        p3_copy(delta).start()
    for delta in range(1, ngy):
        p3_copy(delta).wait_recv()
    for c in range(ngy):
        fac_out[c * chunk : (c + 1) * chunk, :] = fbuf[c]

    for s in range(STEPS):
        for d in order:
            halo_copy(s, d).wait_send()
    for s in range(STEPS + 1):
        for delta in range(1, ngy):
            p1_copy(s, delta).wait_send()
        for delta in range(1, ngx):
            p2_copy(s, delta).wait_send()
    for delta in range(1, ngy):
        p3_copy(delta).wait_send()


def basis_kernel(start, vecs, fac, basis_hbm, factor, result, sem):
    rows, rhs, width = start.shape
    count = STEPS + 1
    lanes = fac[...].T
    for m in range(count):
        factor[m] = lanes[m * count : (m + 1) * count, :]
    group = 8

    def out_copy(c):
        part = pl.ds(pl.multiple_of(c * group, group), group)
        return pltpu.make_async_copy(
            result.at[:, :, part, :], basis_hbm.at[:, :, part, :], sem.at[c]
        )

    def body(c, carry):
        part = pl.ds(pl.multiple_of(c * group, group), group)
        f = fac[part, :]

        def spread(column):
            return jnp.broadcast_to(column, (group, width))

        upper = {
            (m, s): spread(f[:, m * count + s : m * count + s + 1])
            for s in range(count)
            for m in range(s)
        }
        inverse = [
            spread(1.0 / f[:, s * count + s : s * count + s + 1]) for s in range(count)
        ]
        for i in range(rows):
            done = []
            for s in range(count):
                value = start[i, part, :] if s == 0 else vecs[s - 1, i, part, :]
                for m in range(s):
                    value = value - upper[m, s] * done[m]
                value = value * inverse[s]
                done.append(value)
                result[s, i, part, :] = value
        out_copy(c).start()
        return carry

    lax.fori_loop(0, rhs // group, body, 0)
    for c in range(rhs // group):
        out_copy(c).wait()


def on_device(ngx, ngy, blocks, block_cols, live_blocks, send_rows, start, sketch):
    rows, slots, width, _ = blocks.shape
    rhs = start.shape[1]
    sk_rows = sketch.shape[0]
    directions, send_count = send_rows.shape[1:]
    chunk = rhs // ngy
    count = STEPS + 1
    places = rows + directions * send_count + 1
    hbm = pl.BlockSpec(memory_space=pltpu.HBM)
    vmem = pl.BlockSpec(memory_space=pltpu.VMEM)
    dma = pltpu.SemaphoreType.DMA
    vecs, fac = pl.pallas_call(
        functools.partial(power_kernel, ngx, ngy),
        name="power",
        out_shape=[
            jax.ShapeDtypeStruct((STEPS, rows, rhs, width), F32),
            jax.ShapeDtypeStruct((rhs, 128), F32),
        ],
        in_specs=[hbm] * 6,
        out_specs=[vmem, vmem],
        scratch_shapes=[
            pltpu.SMEM(block_cols.shape, jnp.int32),
            pltpu.SMEM(live_blocks.shape, jnp.int32),
            pltpu.SMEM(send_rows.shape[1:], jnp.int32),
            pltpu.VMEM((rows, slots * width, width), BF16),
            pltpu.VMEM((rows, rhs, width), F32),
            pltpu.VMEM((width // 128, sk_rows * rows, 128), F32),
            pltpu.VMEM((rows, 2 * sk_rows, width), BF16),
            *[pltpu.VMEM((places, rhs, width), BF16) for step in range(STEPS)],
            pltpu.VMEM((STEPS, directions, send_count, rhs, width), BF16),
            pltpu.VMEM((count, ngy, chunk, 2 * sk_rows), F32),
            pltpu.VMEM((count, ngy - 1, chunk, 2 * sk_rows), F32),
            pltpu.VMEM((count, ngx, chunk, 2 * sk_rows), F32),
            pltpu.VMEM((ngy, chunk, 128), F32),
            dma((3,)),
            dma((1 + width // 128,)),
            dma((rows,)),
            dma((STEPS, directions)),
            dma((STEPS, directions)),
            dma((count, ngy - 1)),
            dma((count, ngy - 1)),
            dma((count, ngx - 1)),
            dma((count, ngx - 1)),
            dma((ngy - 1,)),
            dma((ngy - 1,)),
        ],
        compiler_params=pltpu.CompilerParams(
            collective_id=0, has_side_effects=True, vmem_limit_bytes=40 * 1024 * 1024
        ),
    )(
        *(
            pltpu.with_memory_space_constraint(array, pltpu.HBM)
            for array in (
                block_cols,
                live_blocks,
                send_rows[0],
                blocks.reshape(rows, slots * width, width),
                start,
                sketch.reshape(sk_rows * rows, width),
            )
        )
    )
    basis, factor = pl.pallas_call(
        basis_kernel,
        name="basis",
        out_shape=[
            jax.ShapeDtypeStruct((count, rows, rhs, width), F32),
            jax.ShapeDtypeStruct((count, count, rhs), F32),
        ],
        in_specs=[vmem, vmem, vmem],
        out_specs=[hbm, vmem],
        scratch_shapes=[
            pltpu.VMEM((count, rows, rhs, width), F32),
            dma((rhs // 8,)),
        ],
        compiler_params=pltpu.CompilerParams(vmem_limit_bytes=16 * 1024 * 1024),
    )(start, vecs, fac)
    return basis, factor


def solution(mesh):
    in_specs = (
        P(("gx", "gy"), None, None, None),
        P(("gx", "gy"), None),
        P(("gx", "gy")),
        P(("gx", "gy"), None, None),
        P(("gx", "gy"), None, None),
        P(None, ("gx", "gy"), None),
    )
    out_specs = (P(None, ("gx", "gy"), None, None), P())
    return jax.shard_map(
        functools.partial(on_device, mesh.shape["gx"], mesh.shape["gy"]),
        mesh=mesh,
        in_specs=in_specs,
        out_specs=out_specs,
        check_vma=False,
    )
```

```python
import functools

import jax
import jax.numpy as jnp
from jax import lax
from jax.experimental import pallas as pl
from jax.experimental.pallas import tpu as pltpu
from jax.sharding import PartitionSpec as P

STEPS = 3
CHUNKS = 2
UNROLL = 8
MESH = pl.DeviceIdType.MESH
F32 = jnp.float32
BF16 = jnp.bfloat16


def contract_last(a, b):
    return lax.dot_general(a, b, (((1,), (1,)), ((), ())), preferred_element_type=F32)


def split_bf16(x):
    high = x.astype(BF16)
    low = (x - high.astype(F32)).astype(BF16)
    return high, low


def power_kernel(
    ngx,
    ngy,
    cols_hbm,
    live_hbm,
    lists_hbm,
    blocks_hbm,
    start_hbm,
    sketch_hbm,
    vecs,
    fac_out,
    cols,
    live,
    lists,
    blk,
    v0,
    sk,
    shl,
    outgoing,
    kept,
    wsend,
    wrecv,
    gxbuf,
    fbuf,
    sem_lists,
    sem_local,
    sem_blk,
    halo_s,
    halo_r,
    p1s,
    p1r,
    p2s,
    p2r,
    p3s,
    p3r,
    *halves,
):
    ext = [halves[s * CHUNKS : (s + 1) * CHUNKS] for s in range(STEPS)]
    rows, rhs, width = v0.shape
    part = rhs // CHUNKS
    slots = cols.shape[1]
    send_count = lists.shape[1]
    sk_rows = shl.shape[1] // 2
    zero_slot = halves[0].shape[0] - 1
    chunk = rhs // ngy
    g, h = lax.axis_index("gx"), lax.axis_index("gy")

    scalar_loads = [
        pltpu.make_async_copy(source, target, sem_lists.at[n])
        for n, (source, target) in enumerate(
            ((lists_hbm, lists), (cols_hbm, cols), (live_hbm, live))
        )
    ]
    for load in scalar_loads:
        load.start()
    load_start = pltpu.make_async_copy(start_hbm, v0, sem_local.at[0])
    load_start.start()
    parts_wide = sk.shape[0]

    def sketch_copy(c):
        return pltpu.make_async_copy(
            sketch_hbm.at[:, pl.ds(c * 128, 128)], sk.at[c], sem_local.at[1 + c]
        )

    for c in range(parts_wide):
        sketch_copy(c).start()

    def block_copy(i):
        return pltpu.make_async_copy(blocks_hbm.at[i], blk.at[i], sem_blk.at[i])

    for i in range(rows):
        block_copy(i).start()

    barrier = pltpu.get_barrier_semaphore()
    for delta in range(1, ngy):
        pl.semaphore_signal(
            barrier, inc=1, device_id={"gy": lax.rem(h + delta, ngy)}, device_id_type=MESH
        )
    for delta in range(1, ngx):
        pl.semaphore_signal(
            barrier, inc=1, device_id={"gx": lax.rem(g + delta, ngx)}, device_id_type=MESH
        )

    for half in halves:
        half[zero_slot] = jnp.zeros((part, width), BF16)

    targets = (
        {"gy": lax.rem(h + 1, ngy)},
        {"gy": lax.rem(h + ngy - 1, ngy)},
        {"gx": lax.rem(g + 1, ngx)},
        {"gx": lax.rem(g + ngx - 1, ngx)},
    )
    order = (2, 3, 0, 1)

    def halo_copy(s, c, d):
        return pltpu.make_async_remote_copy(
            src_ref=outgoing.at[s, c, d],
            dst_ref=ext[s][c].at[pl.ds(rows + d * send_count, send_count)],
            send_sem=halo_s.at[s, c, d],
            recv_sem=halo_r.at[s, c, d],
            device_id=targets[d],
            device_id_type=MESH,
        )

    def span(c):
        return slice(c * part, (c + 1) * part)

    def gather_outgoing(s, c, d):
        for j in range(send_count):
            if s == 0:
                source = v0[lists[d, j], span(c), :]
            else:
                source = vecs[s - 1, lists[d, j], span(c), :]
            outgoing[s, c, d, j] = source.astype(BF16)

    def p1_copy(s, delta):
        to = lax.rem(h + delta, ngy)
        return pltpu.make_async_remote_copy(
            src_ref=wsend.at[s, to],
            dst_ref=wrecv.at[s, delta - 1],
            send_sem=p1s.at[s, delta - 1],
            recv_sem=p1r.at[s, delta - 1],
            device_id={"gy": to},
            device_id_type=MESH,
        )

    def p2_copy(s, delta):
        return pltpu.make_async_remote_copy(
            src_ref=gxbuf.at[s, g],
            dst_ref=gxbuf.at[s, g],
            send_sem=p2s.at[s, delta - 1],
            recv_sem=p2r.at[s, delta - 1],
            device_id={"gx": lax.rem(g + delta, ngx)},
            device_id_type=MESH,
        )

    def p3_copy(delta):
        return pltpu.make_async_remote_copy(
            src_ref=fbuf.at[h],
            dst_ref=fbuf.at[h],
            send_sem=p3s.at[delta - 1],
            recv_sem=p3r.at[delta - 1],
            device_id={"gy": lax.rem(h + delta, ngy)},
            device_id_type=MESH,
        )

    sketched = {}

    def sketch_of(s, c):
        total = jnp.zeros((2 * part, 2 * sk_rows), F32)
        for i in range(rows):
            value = v0[i, span(c), :] if s == 0 else vecs[s - 1, i, span(c), :]
            high, low = split_bf16(value)
            total = total + contract_last(jnp.concatenate([high, low], axis=0), shl[i])
        total = total[:part] + total[part:]
        sketched[s, c] = total[:, :sk_rows] + total[:, sk_rows:]

    def keep_first(pair):
        for c in range(CHUNKS):
            kept[pair, span(c), :] = sketched[2 * pair, c]

    def send_pair(pair):
        for c in range(CHUNKS):
            both = jnp.concatenate(
                [kept[pair, span(c), :], sketched[2 * pair + 1, c]], axis=1
            )
            for k in range(part // chunk):
                wsend[pair, c * (part // chunk) + k] = both[k * chunk : (k + 1) * chunk]
        for delta in range(1, ngy):
            p1_copy(pair, delta).start()

    def finish_gy(s):
        total = wsend[s, h]
        for delta in range(1, ngy):
            p1_copy(s, delta).wait_recv()
            total = total + wrecv[s, delta - 1]
        gxbuf[s, g] = total
        for delta in range(1, ngx):
            p2_copy(s, delta).start()

    units = []
    state = {"fac": jnp.zeros((chunk, 128), F32)}
    lane = lax.broadcasted_iota(jnp.int32, (chunk, 128), 1)

    def put(row, column, value):
        state["fac"] = jnp.where(lane == row * (STEPS + 1) + column, value, state["fac"])

    def finish_gx(pair):
        for delta in range(1, ngx):
            p2_copy(pair, delta).wait_recv()
        total = gxbuf[pair, 0]
        for other in range(1, ngx):
            total = total + gxbuf[pair, other]
        for s in (2 * pair, 2 * pair + 1):
            w = total[:, (s % 2) * sk_rows : (s % 2 + 1) * sk_rows]
            residue = w
            for m in range(s):
                coefficient = jnp.sum(units[m] * w, axis=1, keepdims=True)
                put(m, s, coefficient)
                residue = residue - coefficient * units[m]
            square = jnp.sum(residue * residue, axis=1, keepdims=True)
            length = jnp.sqrt(square + 1e-06)
            put(s, s, length)
            units.append(residue / length)

    for load in scalar_loads:
        load.wait()
    load_start.wait()
    for c in range(CHUNKS):
        for d in order:
            gather_outgoing(0, c, d)
        if c == 0:
            pl.semaphore_wait(barrier, ngx + ngy - 2)
        for d in order:
            halo_copy(0, c, d).start()
    for c in range(CHUNKS):
        for i in range(rows):
            ext[0][c][i] = v0[i, span(c), :].astype(BF16)

    for n in range(parts_wide):
        sketch_copy(n).wait()
        for i in range(rows):
            high, low = split_bf16(sk[n, pl.ds(i, sk_rows, stride=rows), :])
            shl[i, :, n * 128 : (n + 1) * 128] = jnp.concatenate([high, low], axis=0)
    for c in range(CHUNKS):
        sketch_of(0, c)
    keep_first(0)

    for s in range(STEPS):
        for c in range(CHUNKS):
            for d in order:
                halo_copy(s, c, d).wait_recv()

            def row(i):
                parts = [ext[s][c][i]]
                for k in range(1, slots):
                    index = jnp.where(k < live[i], cols[i, k], zero_slot)
                    parts.append(ext[s][c][index])
                product = jnp.dot(
                    jnp.concatenate(parts, axis=1), blk[i], preferred_element_type=F32
                )
                vecs[s, i, span(c), :] = product
                if s + 1 < STEPS:
                    ext[s + 1][c][i] = product.astype(BF16)

            def several(n, carry):
                if s == 0 and c == 0:
                    for u in range(UNROLL):
                        block_copy(n * UNROLL + u).wait()
                for u in range(UNROLL):
                    row(n * UNROLL + u)
                return carry

            lax.fori_loop(0, rows // UNROLL, several, 0)
            if s + 1 < STEPS:
                for d in order:
                    gather_outgoing(s + 1, c, d)
                    halo_copy(s + 1, c, d).start()
            sketch_of(s + 1, c)
        if s % 2 == 0:
            send_pair(s // 2)
        else:
            keep_first((s + 1) // 2)
            finish_gy(0)

    finish_gx(0)
    finish_gy(1)
    finish_gx(1)
    fbuf[h] = state["fac"]
    for delta in range(1, ngy):
        p3_copy(delta).start()
    for delta in range(1, ngy):
        p3_copy(delta).wait_recv()
    for c in range(ngy):
        fac_out[c * chunk : (c + 1) * chunk, :] = fbuf[c]

    for s in range(STEPS):
        for c in range(CHUNKS):
            for d in order:
                halo_copy(s, c, d).wait_send()
    for s in range((STEPS + 1) // 2):
        for delta in range(1, ngy):
            p1_copy(s, delta).wait_send()
        for delta in range(1, ngx):
            p2_copy(s, delta).wait_send()
    for delta in range(1, ngy):
        p3_copy(delta).wait_send()


def basis_kernel(start, vecs, fac, basis_hbm, factor, result, sem):
    rows, rhs, width = start.shape
    count = STEPS + 1
    lanes = fac[...].T
    for m in range(count):
        factor[m] = lanes[m * count : (m + 1) * count, :]
    group = 8

    def out_copy(c):
        part = pl.ds(pl.multiple_of(c * group, group), group)
        return pltpu.make_async_copy(
            result.at[:, :, part, :], basis_hbm.at[:, :, part, :], sem.at[c]
        )

    def body(c, carry):
        part = pl.ds(pl.multiple_of(c * group, group), group)
        f = fac[part, :]

        def spread(column):
            return jnp.broadcast_to(column, (group, width))

        upper = {
            (m, s): spread(f[:, m * count + s : m * count + s + 1])
            for s in range(count)
            for m in range(s)
        }
        inverse = [
            spread(1.0 / f[:, s * count + s : s * count + s + 1]) for s in range(count)
        ]
        for i in range(rows):
            done = []
            for s in range(count):
                value = start[i, part, :] if s == 0 else vecs[s - 1, i, part, :]
                for m in range(s):
                    value = value - upper[m, s] * done[m]
                value = value * inverse[s]
                done.append(value)
                result[s, i, part, :] = value
        out_copy(c).start()
        return carry

    lax.fori_loop(0, rhs // group, body, 0)
    for c in range(rhs // group):
        out_copy(c).wait()


def on_device(ngx, ngy, blocks, block_cols, live_blocks, send_rows, start, sketch):
    rows, slots, width, _ = blocks.shape
    rhs = start.shape[1]
    sk_rows = sketch.shape[0]
    directions, send_count = send_rows.shape[1:]
    chunk = rhs // ngy
    count = STEPS + 1
    pairs = count // 2
    places = rows + directions * send_count + 1
    hbm = pl.BlockSpec(memory_space=pltpu.HBM)
    vmem = pl.BlockSpec(memory_space=pltpu.VMEM)
    dma = pltpu.SemaphoreType.DMA
    vecs, fac = pl.pallas_call(
        functools.partial(power_kernel, ngx, ngy),
        name="power",
        out_shape=[
            jax.ShapeDtypeStruct((STEPS, rows, rhs, width), F32),
            jax.ShapeDtypeStruct((rhs, 128), F32),
        ],
        in_specs=[hbm] * 6,
        out_specs=[vmem, vmem],
        scratch_shapes=[
            pltpu.SMEM(block_cols.shape, jnp.int32),
            pltpu.SMEM(live_blocks.shape, jnp.int32),
            pltpu.SMEM(send_rows.shape[1:], jnp.int32),
            pltpu.VMEM((rows, slots * width, width), BF16),
            pltpu.VMEM((rows, rhs, width), F32),
            pltpu.VMEM((width // 128, sk_rows * rows, 128), F32),
            pltpu.VMEM((rows, 2 * sk_rows, width), BF16),
            pltpu.VMEM(
                (STEPS, CHUNKS, directions, send_count, rhs // CHUNKS, width), BF16
            ),
            pltpu.VMEM((pairs, rhs, sk_rows), F32),
            pltpu.VMEM((pairs, ngy, chunk, 2 * sk_rows), F32),
            pltpu.VMEM((pairs, ngy - 1, chunk, 2 * sk_rows), F32),
            pltpu.VMEM((pairs, ngx, chunk, 2 * sk_rows), F32),
            pltpu.VMEM((ngy, chunk, 128), F32),
            dma((3,)),
            dma((1 + width // 128,)),
            dma((rows,)),
            dma((STEPS, CHUNKS, directions)),
            dma((STEPS, CHUNKS, directions)),
            dma((pairs, ngy - 1)),
            dma((pairs, ngy - 1)),
            dma((pairs, ngx - 1)),
            dma((pairs, ngx - 1)),
            dma((ngy - 1,)),
            dma((ngy - 1,)),
            *[
                pltpu.VMEM((places, rhs // CHUNKS, width), BF16)
                for half in range(STEPS * CHUNKS)
            ],
        ],
        compiler_params=pltpu.CompilerParams(
            collective_id=0, has_side_effects=True, vmem_limit_bytes=40 * 1024 * 1024
        ),
    )(
        *(
            pltpu.with_memory_space_constraint(array, pltpu.HBM)
            for array in (
                block_cols,
                live_blocks,
                send_rows[0],
                blocks.reshape(rows, slots * width, width),
                start,
                sketch.reshape(sk_rows * rows, width),
            )
        )
    )
    basis, factor = pl.pallas_call(
        basis_kernel,
        name="basis",
        out_shape=[
            jax.ShapeDtypeStruct((count, rows, rhs, width), F32),
            jax.ShapeDtypeStruct((count, count, rhs), F32),
        ],
        in_specs=[vmem, vmem, vmem],
        out_specs=[hbm, vmem],
        scratch_shapes=[
            pltpu.VMEM((count, rows, rhs, width), F32),
            dma((rhs // 8,)),
        ],
        compiler_params=pltpu.CompilerParams(vmem_limit_bytes=16 * 1024 * 1024),
    )(start, vecs, fac)
    return basis, factor


def solution(mesh):
    in_specs = (
        P(("gx", "gy"), None, None, None),
        P(("gx", "gy"), None),
        P(("gx", "gy")),
        P(("gx", "gy"), None, None),
        P(("gx", "gy"), None, None),
        P(None, ("gx", "gy"), None),
    )
    out_specs = (P(None, ("gx", "gy"), None, None), P())
    return jax.shard_map(
        functools.partial(on_device, mesh.shape["gx"], mesh.shape["gy"]),
        mesh=mesh,
        in_specs=in_specs,
        out_specs=out_specs,
        check_vma=False,
    )
```

```python
import functools

import jax
import jax.numpy as jnp
from jax import lax
from jax.experimental import pallas as pl
from jax.experimental.pallas import tpu as pltpu
from jax.sharding import PartitionSpec as P

STEPS = 3
CHUNKS = 2
UNROLL = 8
MESH = pl.DeviceIdType.MESH
F32 = jnp.float32
BF16 = jnp.bfloat16


def contract_last(a, b):
    return lax.dot_general(a, b, (((1,), (1,)), ((), ())), preferred_element_type=F32)


def split_bf16(x):
    high = x.astype(BF16)
    low = (x - high.astype(F32)).astype(BF16)
    return high, low


def power_kernel(
    ngx,
    ngy,
    cols_hbm,
    live_hbm,
    lists_hbm,
    blocks_hbm,
    start_hbm,
    sketch_hbm,
    vecs,
    fac_out,
    cols,
    live,
    lists,
    blk,
    v0,
    sk,
    shl,
    outgoing,
    kept,
    wsend,
    wrecv,
    gxbuf,
    fbuf,
    sem_lists,
    sem_local,
    sem_blk,
    halo_s,
    halo_r,
    p1s,
    p1r,
    p2s,
    p2r,
    p3s,
    p3r,
    *halves,
):
    ext = [halves[s * CHUNKS : (s + 1) * CHUNKS] for s in range(STEPS)]
    rows, rhs, width = v0.shape
    part = rhs // CHUNKS
    slots = cols.shape[1]
    send_count = lists.shape[1]
    sk_rows = shl.shape[1] // 2
    zero_slot = halves[0].shape[0] - 1
    chunk = rhs // ngy
    g, h = lax.axis_index("gx"), lax.axis_index("gy")

    scalar_loads = [
        pltpu.make_async_copy(source, target, sem_lists.at[n])
        for n, (source, target) in enumerate(
            ((lists_hbm, lists), (cols_hbm, cols), (live_hbm, live))
        )
    ]
    for load in scalar_loads:
        load.start()
    load_start = pltpu.make_async_copy(start_hbm, v0, sem_local.at[0])
    load_start.start()
    parts_wide = sk.shape[0]

    def sketch_copy(c):
        return pltpu.make_async_copy(
            sketch_hbm.at[:, pl.ds(c * 128, 128)], sk.at[c], sem_local.at[1 + c]
        )

    for c in range(parts_wide):
        sketch_copy(c).start()

    def block_copy(i):
        return pltpu.make_async_copy(blocks_hbm.at[i], blk.at[i], sem_blk.at[i])

    for i in range(rows):
        block_copy(i).start()

    barrier = pltpu.get_barrier_semaphore()
    for delta in range(1, ngy):
        pl.semaphore_signal(
            barrier, inc=1, device_id={"gy": lax.rem(h + delta, ngy)}, device_id_type=MESH
        )
    for delta in range(1, ngx):
        pl.semaphore_signal(
            barrier, inc=1, device_id={"gx": lax.rem(g + delta, ngx)}, device_id_type=MESH
        )

    for half in halves:
        half[zero_slot] = jnp.zeros((part, width), BF16)

    targets = (
        {"gy": lax.rem(h + 1, ngy)},
        {"gy": lax.rem(h + ngy - 1, ngy)},
        {"gx": lax.rem(g + 1, ngx)},
        {"gx": lax.rem(g + ngx - 1, ngx)},
    )
    order = (2, 3, 0, 1)

    def halo_copy(s, c, d):
        return pltpu.make_async_remote_copy(
            src_ref=outgoing.at[s, c, d],
            dst_ref=ext[s][c].at[pl.ds(rows + d * send_count, send_count)],
            send_sem=halo_s.at[s, c, d],
            recv_sem=halo_r.at[s, c, d],
            device_id=targets[d],
            device_id_type=MESH,
        )

    def span(c):
        return slice(c * part, (c + 1) * part)

    def gather_outgoing(s, c, d):
        for j in range(send_count):
            if s == 0:
                source = v0[lists[d, j], span(c), :]
            else:
                source = vecs[s - 1, lists[d, j], span(c), :]
            outgoing[s, c, d, j] = source.astype(BF16)

    def p1_copy(s, delta):
        to = lax.rem(h + delta, ngy)
        return pltpu.make_async_remote_copy(
            src_ref=wsend.at[s, to],
            dst_ref=wrecv.at[s, delta - 1],
            send_sem=p1s.at[s, delta - 1],
            recv_sem=p1r.at[s, delta - 1],
            device_id={"gy": to},
            device_id_type=MESH,
        )

    def p2_copy(s, delta):
        return pltpu.make_async_remote_copy(
            src_ref=gxbuf.at[s, g],
            dst_ref=gxbuf.at[s, g],
            send_sem=p2s.at[s, delta - 1],
            recv_sem=p2r.at[s, delta - 1],
            device_id={"gx": lax.rem(g + delta, ngx)},
            device_id_type=MESH,
        )

    def p3_copy(delta):
        return pltpu.make_async_remote_copy(
            src_ref=fbuf.at[h],
            dst_ref=fbuf.at[h],
            send_sem=p3s.at[delta - 1],
            recv_sem=p3r.at[delta - 1],
            device_id={"gy": lax.rem(h + delta, ngy)},
            device_id_type=MESH,
        )

    sketched = {}

    def sketch_of(s, c):
        total = jnp.zeros((2 * part, 2 * sk_rows), F32)
        for i in range(rows):
            value = v0[i, span(c), :] if s == 0 else vecs[s - 1, i, span(c), :]
            high, low = split_bf16(value)
            total = total + contract_last(jnp.concatenate([high, low], axis=0), shl[i])
        total = total[:part] + total[part:]
        sketched[s, c] = total[:, :sk_rows] + total[:, sk_rows:]

    def keep_first(pair):
        for c in range(CHUNKS):
            kept[pair, span(c), :] = sketched[2 * pair, c]

    def send_pair(pair):
        for c in range(CHUNKS):
            both = jnp.concatenate(
                [kept[pair, span(c), :], sketched[2 * pair + 1, c]], axis=1
            )
            for k in range(part // chunk):
                wsend[pair, c * (part // chunk) + k] = both[k * chunk : (k + 1) * chunk]
        for delta in range(1, ngy):
            p1_copy(pair, delta).start()

    def finish_gy(s):
        total = wsend[s, h]
        for delta in range(1, ngy):
            p1_copy(s, delta).wait_recv()
            total = total + wrecv[s, delta - 1]
        gxbuf[s, g] = total
        for delta in range(1, ngx):
            p2_copy(s, delta).start()

    units = []
    state = {"fac": jnp.zeros((chunk, 128), F32)}
    lane = lax.broadcasted_iota(jnp.int32, (chunk, 128), 1)

    def put(row, column, value):
        state["fac"] = jnp.where(lane == row * (STEPS + 1) + column, value, state["fac"])

    def finish_gx(pair):
        for delta in range(1, ngx):
            p2_copy(pair, delta).wait_recv()
        total = gxbuf[pair, 0]
        for other in range(1, ngx):
            total = total + gxbuf[pair, other]
        for s in (2 * pair, 2 * pair + 1):
            w = total[:, (s % 2) * sk_rows : (s % 2 + 1) * sk_rows]
            residue = w
            for m in range(s):
                coefficient = jnp.sum(units[m] * w, axis=1, keepdims=True)
                put(m, s, coefficient)
                residue = residue - coefficient * units[m]
            square = jnp.sum(residue * residue, axis=1, keepdims=True)
            length = jnp.sqrt(square + 1e-06)
            put(s, s, length)
            if s < STEPS:
                units.append(residue / length)

    for load in scalar_loads:
        load.wait()
    load_start.wait()
    for c in range(CHUNKS):
        if c == 0:
            for d in order:
                gather_outgoing(0, c, d)
            pl.semaphore_wait(barrier, ngx + ngy - 2)
        for d in order:
            if c > 0:
                gather_outgoing(0, c, d)
            halo_copy(0, c, d).start()
    for c in range(CHUNKS):
        for i in range(rows):
            ext[0][c][i] = v0[i, span(c), :].astype(BF16)

    for n in range(parts_wide):
        sketch_copy(n).wait()
        for i in range(rows):
            high, low = split_bf16(sk[n, pl.ds(i, sk_rows, stride=rows), :])
            shl[i, :, n * 128 : (n + 1) * 128] = jnp.concatenate([high, low], axis=0)
    for c in range(CHUNKS):
        sketch_of(0, c)
    keep_first(0)

    for s in range(STEPS):
        for c in range(CHUNKS):
            for d in order:
                halo_copy(s, c, d).wait_recv()

            def row(i):
                parts = [ext[s][c][i]]
                for k in range(1, slots):
                    index = jnp.where(k < live[i], cols[i, k], zero_slot)
                    parts.append(ext[s][c][index])
                product = jnp.dot(
                    jnp.concatenate(parts, axis=1), blk[i], preferred_element_type=F32
                )
                vecs[s, i, span(c), :] = product
                if s + 1 < STEPS:
                    ext[s + 1][c][i] = product.astype(BF16)

            def several(n, carry):
                if s == 0 and c == 0:
                    for u in range(UNROLL):
                        block_copy(n * UNROLL + u).wait()
                for u in range(UNROLL):
                    row(n * UNROLL + u)
                return carry

            lax.fori_loop(0, rows // UNROLL, several, 0)
            if s + 1 < STEPS:
                for d in order:
                    gather_outgoing(s + 1, c, d)
                    halo_copy(s + 1, c, d).start()
            sketch_of(s + 1, c)
        if s % 2 == 0:
            send_pair(s // 2)
        else:
            keep_first((s + 1) // 2)
            finish_gy(0)

    finish_gx(0)
    finish_gy(1)
    finish_gx(1)
    fbuf[h] = state["fac"]
    for delta in range(1, ngy):
        p3_copy(delta).start()
    for delta in range(1, ngy):
        p3_copy(delta).wait_recv()
    for c in range(ngy):
        fac_out[c * chunk : (c + 1) * chunk, :] = fbuf[c]

    for s in range(STEPS):
        for c in range(CHUNKS):
            for d in order:
                halo_copy(s, c, d).wait_send()
    for s in range((STEPS + 1) // 2):
        for delta in range(1, ngy):
            p1_copy(s, delta).wait_send()
        for delta in range(1, ngx):
            p2_copy(s, delta).wait_send()
    for delta in range(1, ngy):
        p3_copy(delta).wait_send()


def basis_kernel(start, vecs, fac, basis_hbm, factor, result, sem):
    rows, rhs, width = start.shape
    count = STEPS + 1
    lanes = fac[...].T
    for m in range(count):
        factor[m] = lanes[m * count : (m + 1) * count, :]
    group = 8

    def out_copy(c):
        part = pl.ds(pl.multiple_of(c * group, group), group)
        return pltpu.make_async_copy(
            result.at[:, :, part, :], basis_hbm.at[:, :, part, :], sem.at[c]
        )

    def body(c, carry):
        part = pl.ds(pl.multiple_of(c * group, group), group)
        f = fac[part, :]

        def spread(column):
            return jnp.broadcast_to(column, (group, width))

        upper = {
            (m, s): spread(f[:, m * count + s : m * count + s + 1])
            for s in range(count)
            for m in range(s)
        }
        inverse = [
            spread(1.0 / f[:, s * count + s : s * count + s + 1]) for s in range(count)
        ]
        for i in range(rows):
            done = []
            for s in range(count):
                value = start[i, part, :] if s == 0 else vecs[s - 1, i, part, :]
                for m in range(s):
                    value = value - upper[m, s] * done[m]
                value = value * inverse[s]
                done.append(value)
                result[s, i, part, :] = value
        out_copy(c).start()
        return carry

    lax.fori_loop(0, rhs // group, body, 0)
    for c in range(rhs // group):
        out_copy(c).wait()


def on_device(ngx, ngy, blocks, block_cols, live_blocks, send_rows, start, sketch):
    rows, slots, width, _ = blocks.shape
    rhs = start.shape[1]
    sk_rows = sketch.shape[0]
    directions, send_count = send_rows.shape[1:]
    chunk = rhs // ngy
    count = STEPS + 1
    pairs = count // 2
    places = rows + directions * send_count + 1
    hbm = pl.BlockSpec(memory_space=pltpu.HBM)
    vmem = pl.BlockSpec(memory_space=pltpu.VMEM)
    dma = pltpu.SemaphoreType.DMA
    vecs, fac = pl.pallas_call(
        functools.partial(power_kernel, ngx, ngy),
        name="power",
        out_shape=[
            jax.ShapeDtypeStruct((STEPS, rows, rhs, width), F32),
            jax.ShapeDtypeStruct((rhs, 128), F32),
        ],
        in_specs=[hbm] * 6,
        out_specs=[vmem, vmem],
        scratch_shapes=[
            pltpu.SMEM(block_cols.shape, jnp.int32),
            pltpu.SMEM(live_blocks.shape, jnp.int32),
            pltpu.SMEM(send_rows.shape[1:], jnp.int32),
            pltpu.VMEM((rows, slots * width, width), BF16),
            pltpu.VMEM((rows, rhs, width), F32),
            pltpu.VMEM((width // 128, sk_rows * rows, 128), F32),
            pltpu.VMEM((rows, 2 * sk_rows, width), BF16),
            pltpu.VMEM(
                (STEPS, CHUNKS, directions, send_count, rhs // CHUNKS, width), BF16
            ),
            pltpu.VMEM((pairs, rhs, sk_rows), F32),
            pltpu.VMEM((pairs, ngy, chunk, 2 * sk_rows), F32),
            pltpu.VMEM((pairs, ngy - 1, chunk, 2 * sk_rows), F32),
            pltpu.VMEM((pairs, ngx, chunk, 2 * sk_rows), F32),
            pltpu.VMEM((ngy, chunk, 128), F32),
            dma((3,)),
            dma((1 + width // 128,)),
            dma((rows,)),
            dma((STEPS, CHUNKS, directions)),
            dma((STEPS, CHUNKS, directions)),
            dma((pairs, ngy - 1)),
            dma((pairs, ngy - 1)),
            dma((pairs, ngx - 1)),
            dma((pairs, ngx - 1)),
            dma((ngy - 1,)),
            dma((ngy - 1,)),
            *[
                pltpu.VMEM((places, rhs // CHUNKS, width), BF16)
                for half in range(STEPS * CHUNKS)
            ],
        ],
        compiler_params=pltpu.CompilerParams(
            collective_id=0, has_side_effects=True, vmem_limit_bytes=40 * 1024 * 1024
        ),
    )(
        *(
            pltpu.with_memory_space_constraint(array, pltpu.HBM)
            for array in (
                block_cols,
                live_blocks,
                send_rows[0],
                blocks.reshape(rows, slots * width, width),
                start,
                sketch.reshape(sk_rows * rows, width),
            )
        )
    )
    basis, factor = pl.pallas_call(
        basis_kernel,
        name="basis",
        out_shape=[
            jax.ShapeDtypeStruct((count, rows, rhs, width), F32),
            jax.ShapeDtypeStruct((count, count, rhs), F32),
        ],
        in_specs=[vmem, vmem, vmem],
        out_specs=[hbm, vmem],
        scratch_shapes=[
            pltpu.VMEM((count, rows, rhs, width), F32),
            dma((rhs // 8,)),
        ],
        compiler_params=pltpu.CompilerParams(vmem_limit_bytes=16 * 1024 * 1024),
    )(start, vecs, fac)
    return basis, factor


def solution(mesh):
    in_specs = (
        P(("gx", "gy"), None, None, None),
        P(("gx", "gy"), None),
        P(("gx", "gy")),
        P(("gx", "gy"), None, None),
        P(("gx", "gy"), None, None),
        P(None, ("gx", "gy"), None),
    )
    out_specs = (P(None, ("gx", "gy"), None, None), P())
    return jax.shard_map(
        functools.partial(on_device, mesh.shape["gx"], mesh.shape["gy"]),
        mesh=mesh,
        in_specs=in_specs,
        out_specs=out_specs,
        check_vma=False,
    )
```
